1024 devices in a mesh: dp: 4 (over x), seq: 16 (over y, core), heads: 16 (over z).
Axes of the slice: x: 4, y: 8, z: 16, core: 2. Of those that a mesh axis runs over, the one named last changes fastest.
Arguments:
- hidden: bfloat16 [4, 4096, 6144], P('dp', 'seq'), may hold values from -6 to 6
- w_gate: bfloat16 [6144, 4096], P('dp', 'heads'), may hold values from -0.078125 to 0.078125
- query_rows: bfloat16 [4, 4096, 4096], P('dp', 'seq', 'heads'), may hold values from -6 to 6
- key_rows: bfloat16 [4, 4096, 4096], P('dp', 'seq', 'heads'), may hold values from -6 to 6
- value_rows: bfloat16 [4, 4096, 4096], P('dp', 'seq', 'heads'), may hold values from -6 to 6
- target: bfloat16 [4, 4096, 4096], P('dp', 'seq', 'heads'), may hold values from -6 to 6
- decay_index: int32 [32], P('heads'), may hold values from 0 to 15
- loss_mask: int32 [4, 4096], P('dp', 'seq'), may hold values from 0 to 1
- doc_reset: int32 [4, 4096], P('dp', 'seq'), may hold values from 0 to 1, as said below
Outputs:
- gated_out: bfloat16 [4, 4096, 4096], P('dp', 'seq', 'heads')
- grad_gate: bfloat16 [4, 4096, 4096], P('dp', 'seq', 'heads')
- grad_query: bfloat16 [4, 4096, 4096], P('dp', 'seq', 'heads')
- grad_key: bfloat16 [4, 4096, 4096], P('dp', 'seq', 'heads')
- grad_value: bfloat16 [4, 4096, 4096], P('dp', 'seq', 'heads')
- mean_loss: float32 [], replicated
The draws below stay inside these ranges and needn't reach their ends.
Inputs may be any that keep to these rules, and one draw needn't show every extreme that they name: `doc_reset`: at most three flags in each sequence.
All inputs are finite; a program needn't handle non-finite values.
Results may differ from the reference program's by a relative error of at most 0.0075.
Values may be sent and summed in bfloat16 or wider, within the bound.
A program may use at most 64 MiB of HBM per device.

```python
import jax
import jax.numpy as jnp
from jax import lax

D = 6144
HD = 128
TABLE = 16
TOK_DEV = 256
HEADS = 32
LEN = 4096
DOCS = 4


def draw_loss_mask(key, part):
    places = jnp.arange(LEN, dtype=jnp.int32)
    limits = 250 + 500 * places // LEN
    rolls = jax.random.randint(key, (DOCS, LEN), 0, 1000, dtype=jnp.int32)
    return (rolls < limits[None, :]).astype(jnp.int32)


def draw_doc_reset(key, part):
    spots = jax.random.randint(key, (DOCS, 3), 0, LEN, dtype=jnp.int32)
    places = jnp.arange(LEN, dtype=jnp.int32)
    hits = jnp.any(spots[:, :, None] == places[None, None, :], axis=1)
    return hits.astype(jnp.int32)


def with_ends(values, stream_key, low, largest):
    index_at = [jax.random.randint(jax.random.fold_in(stream_key, axis), (), 0, length) for axis, length in enumerate(values.shape)]
    main_axis = values.shape.index(max(values.shape))
    beside = index_at[:main_axis] + [(index_at[main_axis] + 1) % values.shape[main_axis]] + index_at[main_axis + 1:]
    return values.at[tuple(index_at)].set(low).at[tuple(beside)].set(largest)


def level_of(stream_key, shape, cuts, smallest, top_value):
    level = 1.0
    for axis_at, parts in cuts:
        steps = jax.random.uniform(jax.random.fold_in(jax.random.fold_in(stream_key, 6), axis_at), (parts,), jnp.float32, smallest / len(cuts), top_value / len(cuts))
        level = level * jnp.repeat(jnp.exp(steps), shape[axis_at] // parts).reshape((-1,) + (1,) * (len(shape) - 1 - axis_at))
    return level


def scatter_about(rng, shape, scale, reach, split=(), kind=jnp.bfloat16):
    entries = jax.random.normal(rng, shape, jnp.float32) * scale
    if len(split) > 0:
        entries = level_of(rng, shape, split, -0.22, 0.18) * entries
    return jnp.clip(entries, min=-reach, max=reach).astype(kind)


def setup_inputs(seed: int = 0) -> dict:
    key_of = jax.random.split(jax.random.key(seed), 10)
    hidden = scatter_about(key_of[0], (DOCS, LEN, D), 1.0, 6.0, ((0, 4), (1, 16)))
    w_gate = scatter_about(key_of[1], (D, HEADS * HD), D ** -0.5, 0.078125, ((0, 4), (1, 16)))
    query_rows = scatter_about(key_of[2], (DOCS, LEN, HEADS * HD), 1.0, 6.0, ((0, 4), (1, 16), (2, 16)))
    key_rows = scatter_about(key_of[3], (DOCS, LEN, HEADS * HD), 1.0, 6.0, ((0, 4), (1, 16), (2, 16)))
    value_rows = scatter_about(key_of[4], (DOCS, LEN, HEADS * HD), 1.0, 6.0, ((0, 4), (1, 16), (2, 16)))
    target = scatter_about(key_of[5], (DOCS, LEN, HEADS * HD), 1.0, 6.0, ((0, 4), (1, 16), (2, 16)))
    decay_index = with_ends(jax.random.randint(key_of[6], (HEADS,), 0, TABLE), jax.random.fold_in(key_of[6], 1), 0, TABLE - 1).astype(jnp.int32)
    loss_mask = draw_loss_mask(jax.random.fold_in(key_of[9], 71), 0)
    doc_reset = draw_doc_reset(jax.random.fold_in(key_of[9], 71), 0)
    return {"hidden": hidden, "w_gate": w_gate, "query_rows": query_rows, "key_rows": key_rows, "value_rows": value_rows, "target": target, "decay_index": decay_index, "loss_mask": loss_mask, "doc_reset": doc_reset}


highest = lax.Precision.HIGHEST
norm_eps = 1e-06

def decay_logs(decay_index, table_len, seq_len):
    table_pos = jnp.arange(table_len, dtype=jnp.float32)
    fast_log = jnp.log(jnp.float32(1.0 / 32.0))
    slow_log = jnp.log(jnp.float32(1.0 / (64.0 * seq_len)))
    table_rates = jnp.exp(fast_log + table_pos / (table_len - 1) * (slow_log - fast_log))
    matches = decay_index[:, None] == jnp.arange(table_len, dtype=jnp.int32)[None, :]
    picked = lax.optimization_barrier(jnp.sum(jnp.where(matches, table_rates[None, :], 0.0), axis=1))
    return -picked

def block_factors(log_decay, reset_block):
    block_len = reset_block.shape[0]
    segment_ids = jnp.cumsum(reset_block).astype(jnp.int32)
    places = jnp.arange(block_len, dtype=jnp.float32)
    causal = places[:, None] >= places[None, :]
    joined = segment_ids[:, None] == segment_ids[None, :]
    allowed = jnp.logical_and(causal, joined)[None, :, :]
    exponents = (places[:, None] - places[None, :])[None, :, :] * log_decay[:, None, None]
    within = jnp.where(allowed, jnp.exp(jnp.where(allowed, exponents, 0.0)), 0.0)
    first_seg = (segment_ids == 0).astype(jnp.float32)
    last_seg = (segment_ids == segment_ids[-1]).astype(jnp.float32)
    opening = jnp.exp((places + 1.0)[None, :] * log_decay[:, None]) * first_seg[None, :]
    closing = jnp.exp((block_len - 1.0 - places)[None, :] * log_decay[:, None]) * last_seg[None, :]
    carry_decay = jnp.exp(block_len * log_decay) * (segment_ids[-1] == 0).astype(jnp.float32)
    return (within, opening, closing, carry_decay)

def forward_local(query3, key3, value3, within, closing):
    scores = jnp.einsum('thd,shd->hts', query3.astype(jnp.float32), key3.astype(jnp.float32))
    weights = (within * scores).astype(jnp.bfloat16)
    weighted = key3.astype(jnp.float32) * jnp.transpose(closing)[:, :, None]
    local_state = jnp.einsum('thd,the->hde', weighted, value3.astype(jnp.float32), precision=highest)
    return (weights, local_state)

def forward_output(weights, query3, value3, opening, state_in):
    inner = jnp.einsum('hts,she->the', weights.astype(jnp.float32), value3.astype(jnp.float32))
    reached = query3.astype(jnp.float32) * jnp.transpose(opening)[:, :, None]
    return inner + jnp.einsum('thd,hde->the', reached, state_in, precision=highest)

def head_norm(attended):
    inv_rms = lax.rsqrt(lax.optimization_barrier(jnp.mean(attended * attended, axis=-1, keepdims=True)) + norm_eps)
    return (attended * inv_rms, inv_rms)

def backward_norm(normed, inv_rms, grad_normed):
    product_mean = lax.optimization_barrier(jnp.mean(grad_normed * normed, axis=-1, keepdims=True))
    return (inv_rms * (grad_normed - normed * product_mean)).astype(jnp.bfloat16)

def grad_state(query3, grad3, opening):
    reached = query3.astype(jnp.float32) * jnp.transpose(opening)[:, :, None]
    return jnp.einsum('thd,the->hde', reached, grad3.astype(jnp.float32), precision=highest)

def backward_block(weights, within, opening, closing, query3, key3, value3, grad3, state_in, state_after):
    grad_f = grad3.astype(jnp.float32)
    key_f = key3.astype(jnp.float32)
    value_f = value3.astype(jnp.float32)
    query_f = query3.astype(jnp.float32)
    open_t = jnp.transpose(opening)[:, :, None]
    close_t = jnp.transpose(closing)[:, :, None]
    mixing = (within * jnp.einsum('the,she->hts', grad_f, value_f)).astype(jnp.bfloat16)
    mixing_f = mixing.astype(jnp.float32)
    grad_query = jnp.einsum('hts,shd->thd', mixing_f, key_f) + jnp.einsum('the,hde->thd', grad_f * open_t, state_in, precision=highest)
    grad_key = jnp.einsum('hts,thd->shd', mixing_f, query_f) + jnp.einsum('the,hde->thd', value_f * close_t, state_after, precision=highest)
    grad_value = jnp.einsum('hts,the->she', weights.astype(jnp.float32), grad_f) + jnp.einsum('thd,hde->the', key_f * close_t, state_after, precision=highest)
    return (grad_query.astype(jnp.bfloat16), grad_key.astype(jnp.bfloat16), grad_value.astype(jnp.bfloat16))

def reference(hidden, w_gate, query_rows, key_rows, value_rows, target, decay_index, loss_mask, doc_reset):
    heads_all = decay_index.shape[0]
    blocks = LEN // TOK_DEV
    log_decay = decay_logs(decay_index, TABLE, LEN)
    count_all = jnp.sum(loss_mask.astype(jnp.float32))
    weight_total = DOCS * LEN / count_all
    zero_state = jnp.zeros((heads_all, HD, HD), jnp.float32)

    def to_blocks(array):
        return array.reshape(DOCS, blocks, TOK_DEV, heads_all, HD)

    def one_doc(inputs):
        hidden_doc, query4, key4, value4, target4, resets2, mask2 = inputs
        gate_pre = jnp.dot(hidden_doc, w_gate, preferred_element_type=jnp.float32)
        gate_val = jax.nn.sigmoid(gate_pre).reshape(blocks, TOK_DEV, heads_all, HD)

        def forward_step(state_in, block):
            query3, key3, value3, reset_block = block
            within, opening, closing, carry_decay = block_factors(log_decay, reset_block)
            weights, local_state = forward_local(query3, key3, value3, within, closing)
            attended = forward_output(weights, query3, value3, opening, state_in)
            return (carry_decay[:, None, None] * state_in + local_state, (attended, state_in))
        final_state, (attended, states_in) = lax.scan(forward_step, zero_state, (query4, key4, value4, resets2))
        normed, inv_rms = head_norm(attended)
        gated = normed * gate_val
        errors = gated - target4.astype(jnp.float32)
        mask4 = mask2.astype(jnp.float32)[:, :, None, None]
        square_sum = jnp.sum(mask4 * errors * errors)
        grad_gated = weight_total * mask4 * errors
        grad_gate = (grad_gated * normed * gate_val * (1.0 - gate_val)).astype(jnp.bfloat16)
        grad_out = backward_norm(normed, inv_rms, grad_gated * gate_val)

        def backward_step(succeeding, block):
            query3, key3, value3, grad3, reset_block, state_in = block
            within, opening, closing, carry_decay = block_factors(log_decay, reset_block)
            weights, local_state = forward_local(query3, key3, value3, within, closing)
            grads = backward_block(weights, within, opening, closing, query3, key3, value3, grad3, state_in, succeeding)
            local_grad = grad_state(query3, grad3, opening)
            return (carry_decay[:, None, None] * succeeding + local_grad, grads)
        final_grad, grads = lax.scan(backward_step, zero_state, (query4, key4, value4, grad_out, resets2, states_in), reverse=True)
        flat = (LEN, heads_all * HD)
        return (gated.astype(jnp.bfloat16).reshape(flat), grad_gate.reshape(flat), grads[0].reshape(flat), grads[1].reshape(flat), grads[2].reshape(flat), square_sum)
    inputs = (hidden, to_blocks(query_rows), to_blocks(key_rows), to_blocks(value_rows), to_blocks(target), doc_reset.reshape(DOCS, blocks, TOK_DEV), loss_mask.reshape(DOCS, blocks, TOK_DEV))
    gated_out, grad_gate, grad_query, grad_key, grad_value, square_sums = lax.map(one_doc, inputs)
    mean_loss = jnp.sum(square_sums) / (2.0 * count_all * (heads_all * HD))
    return (gated_out, grad_gate, grad_query, grad_key, grad_value, mean_loss)
```

```python
import jax
import jax.numpy as jnp
from jax import lax
from jax.sharding import Mesh
from jax.sharding import PartitionSpec as P

TABLE = 16
SEQ = ("seq_0", "seq_1")
DP_SEQ_HEADS = ("dp", "seq_0", "seq_1", "heads")


highest = lax.Precision.HIGHEST
norm_eps = 1e-06


def filled_with(value, identity):
    return jax.tree.map(
        lambda a, e: jnp.broadcast_to(jnp.asarray(e, a.dtype), a.shape), value, identity
    )


def entering(value, axes, combine, identity, reverse):
    before = start = filled_with(value, identity)
    total = value
    for axis in reversed(axes):
        count, position = (lax.axis_size(axis), lax.axis_index(axis))
        pieces = jax.tree.map(lambda part: lax.all_gather(part, axis), total)
        inside, total = (start, start)
        for k in reversed(range(count)) if reverse else range(count):
            passed = k > position if reverse else k < position
            total = combine(total, jax.tree.map(lambda part: part[k], pieces))
            inside = jax.tree.map(lambda new, old: jnp.where(passed, new, old), total, inside)
        before = combine(inside, before)
    return before


def decay_logs(decay_index, table_len, seq_len):
    table_pos = jnp.arange(table_len, dtype=jnp.float32)
    fast_log = jnp.log(jnp.float32(1.0 / 32.0))
    slow_log = jnp.log(jnp.float32(1.0 / (64.0 * seq_len)))
    table_rates = jnp.exp(fast_log + table_pos / (table_len - 1) * (slow_log - fast_log))
    matches = decay_index[:, None] == jnp.arange(table_len, dtype=jnp.int32)[None, :]
    picked = jnp.sum(jnp.where(matches, table_rates[None, :], 0.0), axis=1)
    return -picked


def block_factors(log_decay, reset_block):
    block_len = reset_block.shape[0]
    segment_ids = jnp.cumsum(reset_block)
    places = jnp.arange(block_len, dtype=jnp.float32)
    causal = places[:, None] >= places[None, :]
    joined = segment_ids[:, None] == segment_ids[None, :]
    allowed = jnp.logical_and(causal, joined)[None, :, :]
    exponents = (places[:, None] - places[None, :])[None, :, :] * log_decay[:, None, None]
    within = jnp.where(allowed, jnp.exp(jnp.where(allowed, exponents, 0.0)), 0.0)
    first_seg = (segment_ids == 0).astype(jnp.float32)
    last_seg = (segment_ids == segment_ids[-1]).astype(jnp.float32)
    opening = jnp.exp((places + 1.0)[None, :] * log_decay[:, None]) * first_seg[None, :]
    closing = jnp.exp((block_len - 1.0 - places)[None, :] * log_decay[:, None]) * last_seg[None, :]
    carry_decay = jnp.exp(block_len * log_decay) * (segment_ids[-1] == 0).astype(jnp.float32)
    return (within, opening, closing, carry_decay)


def forward_local(query3, key3, value3, within, closing):
    scores = jnp.einsum("thd,shd->hts", query3, key3, preferred_element_type=jnp.float32)
    weights = (within * scores).astype(jnp.bfloat16)
    weighted = key3.astype(jnp.float32) * jnp.transpose(closing)[:, :, None]
    local_state = jnp.einsum(
        "thd,the->hde", weighted, value3.astype(jnp.float32), precision=highest
    )
    return (weights, local_state)


def forward_output(weights, query3, value3, opening, state_in):
    inner = jnp.einsum("hts,she->the", weights, value3, preferred_element_type=jnp.float32)
    reached = query3.astype(jnp.float32) * jnp.transpose(opening)[:, :, None]
    return inner + jnp.einsum("thd,hde->the", reached, state_in, precision=highest)


def head_norm(attended):
    inv_rms = lax.rsqrt(jnp.mean(attended * attended, axis=-1, keepdims=True) + norm_eps)
    return (attended * inv_rms, inv_rms)


def backward_norm(normed, inv_rms, grad_normed):
    product_mean = jnp.mean(grad_normed * normed, axis=-1, keepdims=True)
    return (inv_rms * (grad_normed - normed * product_mean)).astype(jnp.bfloat16)


def grad_state(query3, grad3, opening):
    reached = query3.astype(jnp.float32) * jnp.transpose(opening)[:, :, None]
    return jnp.einsum("thd,the->hde", reached, grad3.astype(jnp.float32), precision=highest)


def backward_block(
    weights, within, opening, closing, query3, key3, value3, grad3, state_in, state_after
):
    open_t = jnp.transpose(opening)[:, :, None]
    close_t = jnp.transpose(closing)[:, :, None]
    mixing = (
        within * jnp.einsum("the,she->hts", grad3, value3, preferred_element_type=jnp.float32)
    ).astype(jnp.bfloat16)
    grad_query = jnp.einsum(
        "hts,shd->thd", mixing, key3, preferred_element_type=jnp.float32
    ) + jnp.einsum("the,hde->thd", grad3.astype(jnp.float32) * open_t, state_in, precision=highest)
    grad_key = jnp.einsum(
        "hts,thd->shd", mixing, query3, preferred_element_type=jnp.float32
    ) + jnp.einsum(
        "the,hde->thd", value3.astype(jnp.float32) * close_t, state_after, precision=highest
    )
    grad_value = jnp.einsum(
        "hts,the->she", weights, grad3, preferred_element_type=jnp.float32
    ) + jnp.einsum(
        "thd,hde->the", key3.astype(jnp.float32) * close_t, state_after, precision=highest
    )
    return (
        grad_query.astype(jnp.bfloat16),
        grad_key.astype(jnp.bfloat16),
        grad_value.astype(jnp.bfloat16),
    )


def chain_blocks(earlier, succeeding):
    return (earlier[0] * succeeding[0], succeeding[0][:, None, None] * earlier[1] + succeeding[1])


def local(
    hidden, w_gate, query_rows, key_rows, value_rows, target, decay_index, loss_mask, doc_reset
):
    tokens_dev = hidden.shape[1]
    heads_dev = decay_index.shape[0]
    head_size = query_rows.shape[2] // heads_dev
    seq_count = lax.axis_size(SEQ)
    log_decay = decay_logs(decay_index, TABLE, tokens_dev * seq_count)
    mask_rows = loss_mask[0].astype(jnp.float32)
    count_dev = jnp.sum(mask_rows)
    columns = hidden[0]
    gate_pre = jnp.dot(
        columns,
        lax.all_gather(w_gate, "dp", axis=0, tiled=True),
        preferred_element_type=jnp.float32,
    )
    gate_val = jax.nn.sigmoid(gate_pre).reshape(tokens_dev, heads_dev, head_size)
    query3 = query_rows[0].reshape(tokens_dev, heads_dev, head_size)
    key3 = key_rows[0].reshape(tokens_dev, heads_dev, head_size)
    value3 = value_rows[0].reshape(tokens_dev, heads_dev, head_size)
    target3 = target[0].reshape(tokens_dev, heads_dev, head_size)
    within, opening, closing, carry_decay = block_factors(log_decay, doc_reset[0])
    weights, local_state = forward_local(query3, key3, value3, within, closing)
    identity = (
        jnp.ones((heads_dev,), jnp.float32),
        jnp.zeros((heads_dev, head_size, head_size), jnp.float32),
    )
    state_in = entering((carry_decay, local_state), SEQ, chain_blocks, identity, False)[1]
    attended = forward_output(weights, query3, value3, opening, state_in)
    normed, inv_rms = head_norm(attended)
    gated = normed * gate_val
    errors = gated - target3.astype(jnp.float32)
    mask3 = mask_rows[:, None, None]
    square_sum = jnp.sum(mask3 * errors * errors)
    totals = lax.psum(jnp.stack([count_dev, square_sum]), DP_SEQ_HEADS)
    count_sum, error_all = (totals[0], totals[1])
    count_all = count_sum / lax.axis_size("heads")
    weight_total = lax.axis_size("dp") * seq_count * tokens_dev / count_all
    grad_gated = weight_total * mask3 * errors
    grad_gate = (grad_gated * normed * gate_val * (1.0 - gate_val)).astype(jnp.bfloat16)
    grad_out = backward_norm(normed, inv_rms, grad_gated * gate_val)
    local_grad = grad_state(query3, grad_out, opening)
    state_after = entering((carry_decay, local_grad), SEQ, chain_blocks, identity, True)[1]
    grad_query, grad_key, grad_value = backward_block(
        weights, within, opening, closing, query3, key3, value3, grad_out, state_in, state_after
    )
    mean_loss = error_all / (2.0 * count_all * (heads_dev * lax.axis_size("heads") * head_size))
    flat = (1, tokens_dev, heads_dev * head_size)
    return (
        gated.astype(jnp.bfloat16).reshape(flat),
        grad_gate.reshape(flat),
        grad_query.reshape(flat),
        grad_key.reshape(flat),
        grad_value.reshape(flat),
        mean_loss,
    )


def solution(mesh):
    finer = Mesh(
        mesh.devices.reshape(mesh.shape["dp"], 8, 2, mesh.shape["heads"]),
        ("dp", "seq_0", "seq_1", "heads"),
    )
    placed = (
        P("dp", SEQ, None),
        P("dp", "heads"),
        P("dp", SEQ, "heads"),
        P("dp", SEQ, "heads"),
        P("dp", SEQ, "heads"),
        P("dp", SEQ, "heads"),
        P("heads"),
        P("dp", SEQ),
        P("dp", SEQ),
    )
    return jax.shard_map(
        local,
        mesh=finer,
        in_specs=placed,
        out_specs=(
            P("dp", SEQ, "heads"),
            P("dp", SEQ, "heads"),
            P("dp", SEQ, "heads"),
            P("dp", SEQ, "heads"),
            P("dp", SEQ, "heads"),
            P(),
        ),
        check_vma=False,
    )
```

```python
import functools

import jax
import jax.numpy as jnp
import numpy as np
from jax import lax
from jax.experimental import pallas as pl
from jax.experimental.pallas import tpu as pltpu
from jax.sharding import PartitionSpec as P

TABLE = 16
NORM_EPS = 1e-06
CHUNKS = 4
F32, BF16 = jnp.float32, jnp.bfloat16
NN, NT, TN = ((1,), (0,)), ((1,), (1,)), ((0,), (0,))


def mm(a, b, dims=NN):
    return lax.dot_general(a, b, (dims, ((), ())), preferred_element_type=F32)


def split(x):
    hi = x.astype(BF16)
    return hi, (x - hi.astype(F32)).astype(BF16)


def farthest_first(n):
    return sorted(range(1, n), key=lambda d: -min(d, n - d))


def exchange(src, dst, axis, n, me, send, recv):
    copies = []
    for d in farthest_first(n):
        peer = lax.rem(me + d, n)
        copies.append(
            pltpu.make_async_remote_copy(
                src_ref=src(peer),
                dst_ref=dst(me),
                send_sem=send.at[d],
                recv_sem=recv.at[d],
                device_id={axis: peer},
                device_id_type=pl.DeviceIdType.MESH,
            )
        )
    return copies


def start(copies):
    for copy in copies:
        copy.start()


def arrived(copies):
    for copy in copies:
        copy.wait_recv()


def sent(copies):
    for copy in copies:
        copy.wait_send()


def kernel(
    n_dp, n_seq, n_heads,
    idx, mask_hbm, reset_hbm, hid_hbm, w_hbm, q_hbm, k_hbm, v_hbm, t_hbm,
    gated_ref, ggate_ref, gq_ref, gk_ref, gv_ref, loss_ref,
    hid, wbuf, qb, kb, vb, tb, mk, rs, gate_acc,
    within, pbuf, opening, closing, inner, gout, gkp, gvp,
    info, cnt, l1, l2, l3, s1src, s1, s2src, s2, g1src, g1, g2src, g2,
    loc, w_send, w_recv, sib_send, sib_recv, seq_send, seq_recv, dp_send, dp_recv, z_send, z_recv,
):
    x, b, z = lax.axis_index("dp"), lax.axis_index("seq"), lax.axis_index("heads")
    T = qb.shape[0]
    hd = gout.shape[2]
    heads_dev = gout.shape[0]
    depth = w_hbm.shape[0]
    piece = depth // 2 // CHUNKS
    rows = hd // n_seq
    core = lax.rem(b, 2)
    sibling = b + 1 - 2 * core
    ahead = lax.rem(x + 1 + 2 * core, n_dp)
    back = lax.rem(x + 3 - 2 * core, n_dp)
    across = lax.rem(x + 2, n_dp)

    barrier = pltpu.get_barrier_semaphore()
    for axis, n, me in (("seq", n_seq, b), ("dp", n_dp, x), ("heads", n_heads, z)):
        for d in farthest_first(n):
            pl.semaphore_signal(
                barrier, inc=1, device_id={axis: lax.rem(me + d, n)}, device_id_type=pl.DeviceIdType.MESH
            )
    local = [
        pltpu.make_async_copy(s, d, loc.at[i])
        for i, (s, d) in enumerate((
            (reset_hbm, rs), (mask_hbm, mk), (k_hbm.at[0], kb), (v_hbm.at[0], vb), (q_hbm.at[0], qb),
            (w_hbm, wbuf.at[x]), (hid_hbm.at[0], hid), (t_hbm.at[0], tb),
        ))
    ]
    start(local)

    local[0].wait()
    local[1].wait()
    row_i = lax.broadcasted_iota(jnp.int32, (T, T), 0)
    col_i = lax.broadcasted_iota(jnp.int32, (T, T), 1)
    lower = (col_i <= row_i).astype(F32).astype(BF16)
    upper = (row_i <= col_i).astype(F32).astype(BF16)
    flags = jnp.broadcast_to(rs[...].astype(F32), (T, T)).astype(BF16)
    seg_col = mm(lower, flags, NT)
    seg_row = mm(flags, upper)
    last = seg_col[T - 1:T, :hd]
    allowed = jnp.logical_and(col_i <= row_i, seg_col == seg_row)
    masks = jnp.broadcast_to(mk[...].astype(F32), (hd, T)).astype(BF16)
    mask_col = mm((col_i == row_i).astype(F32).astype(BF16), masks, NT)
    count_dev = mm(masks[:8], jnp.ones((T, hd), BF16))
    gap = (row_i - col_i).astype(F32)
    place = row_i[:, :hd].astype(F32)
    fast = float(np.log(np.float32(1.0 / 32.0)))
    slow = float(np.log(np.float32(1.0 / (64.0 * T * n_seq))))
    carries = []
    for h in range(heads_dev):
        entry = jnp.full((1, T), idx[h].astype(F32), F32)
        ell = -jnp.exp(fast + entry / (TABLE - 1) * (slow - fast))
        within[h] = jnp.where(allowed, jnp.exp(gap * ell), 0.0)
        ell = ell[:, :hd]
        opening[h] = jnp.where(seg_col[:, :hd] == 0.0, jnp.exp((place + 1.0) * ell), 0.0)
        closing[h] = jnp.where(seg_col[:, :hd] == last, jnp.exp((T - 1.0 - place) * ell), 0.0)
        carries.append(jnp.exp(T * ell))
    tile_row = lax.broadcasted_iota(jnp.int32, (8, hd), 0)
    info[b] = jnp.where(tile_row < 4, jnp.broadcast_to((last == 0.0).astype(F32), (8, hd)), count_dev)

    def head(ref, h):
        return ref[:, h * hd:(h + 1) * hd]

    local[2].wait()
    local[3].wait()
    for h in range(heads_dev):
        hi, lo = split(head(kb, h).astype(F32) * closing[h])
        value = head(vb, h)
        s1src[:, h] = (mm(hi, value, TN) + mm(lo, value, TN)).reshape(n_seq, rows, hd)

    pl.semaphore_wait(barrier, n_seq + n_dp + n_heads - 3)

    def w_piece(shard, half, i):
        return wbuf.at[shard, pl.ds(pl.multiple_of(half * (depth // 2) + i * piece, piece), piece), :]

    def w_copy(src, shard, i, route, peer):
        return pltpu.make_async_remote_copy(
            src_ref=src, dst_ref=w_piece(shard, core, i), send_sem=w_send.at[route, i], recv_sem=w_recv.at[route, i],
            device_id={"dp": peer}, device_id_type=pl.DeviceIdType.MESH,
        )

    def w_own(i):
        return w_hbm.at[pl.ds(pl.multiple_of(core * (depth // 2) + i * piece, piece), piece), :]

    def w_pass(shard, i, route):
        return pltpu.make_async_remote_copy(
            src_ref=w_piece(shard, core, i), dst_ref=w_piece(shard, core, i),
            send_sem=sib_send.at[route, i], recv_sem=sib_recv.at[route, i],
            device_id={"seq": sibling}, device_id_type=pl.DeviceIdType.MESH,
        )

    steps = range(CHUNKS)
    to_ahead = [w_copy(w_own(i), x, i, 0, ahead) for i in steps]
    to_back = [w_copy(w_own(i), x, i, 1, back) for i in steps]
    onward = [w_copy(w_piece(back, core, i), back, i, 2, ahead) for i in steps]
    passes = [[w_pass(shard, i, r) for i in steps] for r, shard in enumerate((back, ahead, across))]

    infos = exchange(lambda p: info.at[b], lambda me: info.at[me], "seq", n_seq, b, seq_send.at[0], seq_recv.at[0])
    states = exchange(lambda p: s1src.at[p], lambda me: s1.at[me], "seq", n_seq, b, seq_send.at[1], seq_recv.at[1])
    start(infos)
    start(states)
    for i in steps:
        to_ahead[i].start()
        to_back[i].start()
    s1[b] = s1src[b]

    local[4].wait()
    for h in range(heads_dev):
        scores = mm(head(qb, h), head(kb, h), NT)
        pbuf[h] = (within[h] * scores).astype(BF16)
        inner[h] = mm(pbuf[h], head(vb, h))

    def w_step(i):
        to_ahead[i].wait_recv()
        onward[i].start()
        passes[0][i].start()
        to_back[i].wait_recv()
        passes[1][i].start()

    def gate_part(shard, first=False):
        columns = pl.ds(pl.multiple_of(shard * depth, depth), depth)
        part = mm(hid[:, columns], wbuf[shard])
        gate_acc[...] = part if first else gate_acc[...] + part

    local[5].wait()
    local[6].wait()
    gate_part(x, first=True)
    w_step(0)
    arrived(infos)
    keep = [info[j, 0:1] for j in range(n_seq)]
    cnt[x] = functools.reduce(jnp.add, [info[j, 4:8] for j in range(n_seq)])
    counts = exchange(lambda p: cnt.at[x], lambda me: cnt.at[me], "dp", n_dp, x, dp_send.at[0], dp_recv.at[0])
    start(counts)

    def scan(source, result, order):
        for h in range(heads_dev):
            state = jnp.zeros((rows, hd), F32)
            for j in order:
                result[j, h] = state
                state = carries[h] * keep[j] * state + source[j, h]

    arrived(states)
    scan(s1, s2src, range(n_seq))
    states_in = exchange(lambda p: s2src.at[p], lambda me: s2.at[me], "seq", n_seq, b, seq_send.at[2], seq_recv.at[2])
    start(states_in)
    s2[b] = s2src[b]
    for i in steps[1:]:
        w_step(i)
    local[7].wait()
    arrived(states_in)
    state_in = [split(s2[:, h].reshape(hd, hd)) for h in range(heads_dev)]
    for h in range(heads_dev):
        query = head(qb, h)
        inner[h] = inner[h] + opening[h] * (mm(query, state_in[h][0]) + mm(query, state_in[h][1]))
    arrived(passes[1])
    gate_part(back)
    arrived(passes[0])
    gate_part(ahead)
    for i in steps:
        onward[i].wait_recv()
        passes[2][i].start()
    arrived(passes[2])
    gate_part(across)
    arrived(counts)
    count = functools.reduce(jnp.add, [cnt[j] for j in range(n_dp)])[0:1]
    scale = n_dp * n_seq * T / count

    square = jnp.zeros((8, hd), F32)
    for h in range(heads_dev):
        attended = inner[h]
        inv = lax.rsqrt(jnp.mean(attended * attended, axis=-1, keepdims=True) + NORM_EPS)
        normed = attended * inv
        gate = jax.nn.sigmoid(gate_acc[:, h * hd:(h + 1) * hd])
        gated = normed * gate
        errors = gated - head(tb, h).astype(F32)
        masked = mask_col * errors
        square = square + jnp.sum((masked * errors).reshape(T // 8, 8, hd), axis=0)
        grad_gated = scale * masked
        dn = grad_gated * gate
        gated_ref[0, :, h * hd:(h + 1) * hd] = gated.astype(BF16)
        ggate_ref[0, :, h * hd:(h + 1) * hd] = (dn * normed * (1.0 - gate)).astype(BF16)
        product = jnp.mean(dn * normed, axis=-1, keepdims=True)
        gout[h] = (inv * (dn - normed * product)).astype(BF16)
    l1[b] = square
    losses = exchange(lambda p: l1.at[b], lambda me: l1.at[me], "seq", n_seq, b, seq_send.at[3], seq_recv.at[3])
    start(losses)
    for h in range(heads_dev):
        hi, lo = split(head(qb, h).astype(F32) * opening[h])
        g1src[:, h] = (mm(hi, gout[h], TN) + mm(lo, gout[h], TN)).reshape(n_seq, rows, hd)
    grads = exchange(lambda p: g1src.at[p], lambda me: g1.at[me], "seq", n_seq, b, seq_send.at[4], seq_recv.at[4])
    start(grads)
    g1[b] = g1src[b]
    for h in range(heads_dev):
        grad = gout[h]
        mixing = (within[h] * mm(grad, head(vb, h), NT)).astype(BF16)
        carried = mm(grad, state_in[h][0], NT) + mm(grad, state_in[h][1], NT)
        gq_ref[0, :, h * hd:(h + 1) * hd] = (mm(mixing, head(kb, h)) + opening[h] * carried).astype(BF16)
        gkp[h] = mm(mixing, head(qb, h), TN)
        gvp[h] = mm(pbuf[h], grad, TN)
    arrived(losses)
    l2[x] = functools.reduce(jnp.add, [l1[j] for j in range(n_seq)])
    losses_dp = exchange(lambda p: l2.at[x], lambda me: l2.at[me], "dp", n_dp, x, dp_send.at[1], dp_recv.at[1])
    start(losses_dp)
    arrived(grads)
    scan(g1, g2src, range(n_seq - 1, -1, -1))
    states_after = exchange(lambda p: g2src.at[p], lambda me: g2.at[me], "seq", n_seq, b, seq_send.at[5], seq_recv.at[5])
    start(states_after)
    g2[b] = g2src[b]
    arrived(losses_dp)
    l3[z] = functools.reduce(jnp.add, [l2[j] for j in range(n_dp)])
    losses_z = exchange(lambda p: l3.at[z], lambda me: l3.at[me], "heads", n_heads, z, z_send, z_recv)
    start(losses_z)
    arrived(states_after)
    for h in range(heads_dev):
        hi, lo = split(g2[:, h].reshape(hd, hd))
        value, key = head(vb, h), head(kb, h)
        gk_ref[0, :, h * hd:(h + 1) * hd] = (gkp[h] + closing[h] * (mm(value, hi, NT) + mm(value, lo, NT))).astype(BF16)
        gv_ref[0, :, h * hd:(h + 1) * hd] = (gvp[h] + closing[h] * (mm(key, hi) + mm(key, lo))).astype(BF16)
    arrived(losses_z)
    total = functools.reduce(jnp.add, [l3[j] for j in range(n_heads)])
    loss_ref[0, 0] = jnp.sum(total / (2.0 * count * (heads_dev * n_heads * hd)))

    for copies in (to_ahead, to_back, onward, *passes, infos, states, counts, states_in, losses, grads, losses_dp, states_after, losses_z):
        sent(copies)


def local_step(sizes, hidden, w_gate, query_rows, key_rows, value_rows, target, decay_index, loss_mask, doc_reset):
    n_dp, n_seq, n_heads = sizes
    T, D = hidden.shape[1:]
    depth, width = w_gate.shape
    heads_dev = decay_index.shape[0]
    hd = width // heads_dev
    rows = hd // n_seq
    any_spec = pl.BlockSpec(memory_space=pl.ANY)
    out = jax.ShapeDtypeStruct((1, T, width), BF16)
    state = pltpu.VMEM((n_seq, heads_dev, rows, hd), F32)
    scratch = [
        pltpu.VMEM((T, D), BF16), pltpu.VMEM((n_dp, depth, width), BF16),
        *[pltpu.VMEM((T, width), BF16)] * 4,
        pltpu.VMEM((1, T), jnp.int32), pltpu.VMEM((1, T), jnp.int32), pltpu.VMEM((T, width), F32),
        pltpu.VMEM((heads_dev, T, T), F32), pltpu.VMEM((heads_dev, T, T), BF16),
        pltpu.VMEM((heads_dev, T, hd), F32), pltpu.VMEM((heads_dev, T, hd), F32), pltpu.VMEM((heads_dev, T, hd), F32),
        pltpu.VMEM((heads_dev, T, hd), BF16), pltpu.VMEM((heads_dev, T, hd), F32), pltpu.VMEM((heads_dev, T, hd), F32),
        pltpu.VMEM((n_seq, 8, hd), F32), pltpu.VMEM((n_dp, 4, hd), F32),
        pltpu.VMEM((n_seq, 8, hd), F32), pltpu.VMEM((n_dp, 8, hd), F32), pltpu.VMEM((n_heads, 8, hd), F32),
        *[state] * 8,
        pltpu.SemaphoreType.DMA((8,)),
        pltpu.SemaphoreType.DMA((3, CHUNKS)), pltpu.SemaphoreType.DMA((3, CHUNKS)),
        pltpu.SemaphoreType.DMA((3, CHUNKS)), pltpu.SemaphoreType.DMA((3, CHUNKS)),
        pltpu.SemaphoreType.DMA((6, n_seq)), pltpu.SemaphoreType.DMA((6, n_seq)),
        pltpu.SemaphoreType.DMA((2, n_dp)), pltpu.SemaphoreType.DMA((2, n_dp)),
        pltpu.SemaphoreType.DMA((n_heads,)), pltpu.SemaphoreType.DMA((n_heads,)),
    ]
    vmem, smem = pl.BlockSpec(memory_space=pltpu.VMEM), pl.BlockSpec(memory_space=pltpu.SMEM)
    *results, loss = pl.pallas_call(
        functools.partial(kernel, n_dp, n_seq, n_heads),
        out_shape=[out] * 5 + [jax.ShapeDtypeStruct((1, 1), F32)],
        in_specs=[smem] + [any_spec] * 8,
        out_specs=[vmem] * 5 + [smem],
        scratch_shapes=scratch,
        compiler_params=pltpu.CompilerParams(collective_id=0, has_side_effects=True),
        name="layer",
    )(decay_index, loss_mask, doc_reset, hidden, w_gate, query_rows, key_rows, value_rows, target)
    return (*results, loss.reshape(()))


def solution(mesh):
    sizes = tuple(mesh.shape[a] for a in ("dp", "seq", "heads"))
    rows = P("dp", "seq", "heads")
    return jax.shard_map(
        functools.partial(local_step, sizes),
        mesh=mesh,
        in_specs=(P("dp", "seq", None), P("dp", "heads"), rows, rows, rows, rows, P("heads"), P("dp", "seq"), P("dp", "seq")),
        out_specs=(rows, rows, rows, rows, rows, P()),
        check_vma=False,
    )
```

```python
import functools

import jax
import jax.numpy as jnp
import numpy as np
from jax import lax
from jax.experimental import pallas as pl
from jax.experimental.pallas import tpu as pltpu
from jax.sharding import PartitionSpec as P

TABLE = 16
NORM_EPS = 1e-06
CHUNKS = 4
STATE = jnp.bfloat16
F32, BF16 = jnp.float32, jnp.bfloat16
NN, NT, TN = ((1,), (0,)), ((1,), (1,)), ((0,), (0,))


def mm(a, b, dims=NN):
    return lax.dot_general(a, b, (dims, ((), ())), preferred_element_type=F32)


def split(x):
    hi = x.astype(BF16)
    return hi, (x - hi.astype(F32)).astype(BF16)


def farthest_first(n):
    return sorted(range(1, n), key=lambda d: -min(d, n - d))


def exchange(src, dst, axis, n, me, send, recv):
    copies = []
    for d in farthest_first(n):
        peer = lax.rem(me + d, n)
        copies.append(
            pltpu.make_async_remote_copy(
                src_ref=src(peer),
                dst_ref=dst(me),
                send_sem=send.at[d],
                recv_sem=recv.at[d],
                device_id={axis: peer},
                device_id_type=pl.DeviceIdType.MESH,
            )
        )
    return copies


def signal(sem, axis, peer):
    pl.semaphore_signal(sem, inc=1, device_id={axis: peer}, device_id_type=pl.DeviceIdType.MESH)


def start(copies):
    for copy in copies:
        copy.start()


def arrived(copies):
    for copy in copies:
        copy.wait_recv()


def sent(copies):
    for copy in copies:
        copy.wait_send()


def kernel(
    n_dp, n_seq, n_heads,
    idx, mask_hbm, reset_hbm, hid_hbm, w_hbm, q_hbm, k_hbm, v_hbm, t_hbm,
    gated_ref, ggate_ref, gq_ref, gk_ref, gv_ref, loss_ref,
    hid, wbuf, qb, kb, vb, tb, mk, rs, gate_acc, mask_col,
    within, pbuf, opening, closing, inner, gout, gkp, gvp,
    info, cnt, l1, l2, l3, s1src, s1, s2src, s2, g1src, g1, g2src, g2,
    loc, w_send, w_recv, sib_send, sib_recv, seq_send, seq_recv, dp_send, dp_recv, z_send, z_recv, ready,
):
    x, b, z = lax.axis_index("dp"), lax.axis_index("seq"), lax.axis_index("heads")
    T = qb.shape[0]
    hd = gout.shape[2]
    heads_dev = gout.shape[0]
    depth = w_hbm.shape[0]
    piece = depth // 2 // CHUNKS
    rows = hd // n_seq
    core = lax.rem(b, 2)
    sibling = b + 1 - 2 * core
    ahead = lax.rem(x + 1 + 2 * core, n_dp)
    back = lax.rem(x + 3 - 2 * core, n_dp)
    across = lax.rem(x + 2, n_dp)

    barrier = pltpu.get_barrier_semaphore()
    for axis, n, me, reach in (("seq", n_seq, b, n_seq), ("dp", n_dp, x, n_dp), ("heads", n_heads, z, 1)):
        for d in farthest_first(n):
            if min(d, n - d) <= reach:
                signal(barrier, axis, lax.rem(me + d, n))
    local = [
        pltpu.make_async_copy(s, d, loc.at[i])
        for i, (s, d) in enumerate((
            (reset_hbm, rs), (mask_hbm, mk), (k_hbm.at[0], kb), (v_hbm.at[0], vb), (q_hbm.at[0], qb),
            (w_hbm, wbuf.at[x]), (hid_hbm.at[0], hid), (t_hbm.at[0], tb),
        ))
    ]
    start(local)

    local[0].wait()
    local[1].wait()
    row_i = lax.broadcasted_iota(jnp.int32, (T, T), 0)
    col_i = lax.broadcasted_iota(jnp.int32, (T, T), 1)
    lower = (col_i <= row_i).astype(F32).astype(BF16)
    upper = (row_i <= col_i).astype(F32).astype(BF16)
    flags = jnp.broadcast_to(rs[...].astype(F32), (T, T)).astype(BF16)
    seg_col = mm(lower, flags, NT)
    last = seg_col[T - 1:T, :hd]
    masks = jnp.broadcast_to(mk[...].astype(F32), (hd, T)).astype(BF16)
    count_dev = mm(masks[:8], jnp.ones((T, hd), BF16))
    place = row_i[:, :hd].astype(F32)
    fast = float(np.log(np.float32(1.0 / 32.0)))
    slow = float(np.log(np.float32(1.0 / (64.0 * T * n_seq))))
    ells, carries = [], []
    for h in range(heads_dev):
        entry = jnp.full((1, T), idx[h].astype(F32), F32)
        ell = -jnp.exp(fast + entry / (TABLE - 1) * (slow - fast))
        ells.append(ell)
        ell = ell[:, :hd]
        closing[h] = jnp.where(seg_col[:, :hd] == last, jnp.exp((T - 1.0 - place) * ell), 0.0)
        carries.append(jnp.broadcast_to(jnp.exp(T * ell), (rows, hd)))
    tile_row = lax.broadcasted_iota(jnp.int32, (8, hd), 0)
    info[b] = jnp.where(tile_row < 4, jnp.broadcast_to((last == 0.0).astype(F32), (8, hd)), count_dev)

    def head(ref, h):
        return ref[:, h * hd:(h + 1) * hd]

    local[2].wait()
    local[3].wait()
    def pack(ref, parts):
        ref[...] = jnp.concatenate([p.reshape(n_seq, rows, hd) for p in parts], axis=1).astype(ref.dtype)

    def unpack(ref, h):
        state = ref[...].astype(F32)[:, h * rows:(h + 1) * rows].reshape(hd, hd)
        return (state.astype(BF16),) if ref.dtype == BF16 else split(state)

    def times(a, parts, dims=NN):
        return functools.reduce(jnp.add, [mm(a, p, dims) for p in parts])

    pack(s1src, [
        functools.reduce(jnp.add, [mm(part, head(vb, h), TN) for part in split(head(kb, h).astype(F32) * closing[h])])
        for h in range(heads_dev)
    ])

    pl.semaphore_wait(barrier, n_seq + n_dp)

    def wave_signal(d, i):
        for peer in (z + d, z + n_heads - d):
            signal(ready.at[i], "heads", lax.rem(peer, n_heads))

    wave_signal(1, 0)

    def w_piece(shard, half, i):
        return wbuf.at[shard, pl.ds(pl.multiple_of(half * (depth // 2) + i * piece, piece), piece), :]

    def w_copy(src, shard, i, route, peer):
        return pltpu.make_async_remote_copy(
            src_ref=src, dst_ref=w_piece(shard, core, i), send_sem=w_send.at[route, i], recv_sem=w_recv.at[route, i],
            device_id={"dp": peer}, device_id_type=pl.DeviceIdType.MESH,
        )

    def w_own(i):
        return w_hbm.at[pl.ds(pl.multiple_of(core * (depth // 2) + i * piece, piece), piece), :]

    def w_pass(shard, i, route):
        return pltpu.make_async_remote_copy(
            src_ref=w_piece(shard, core, i), dst_ref=w_piece(shard, core, i),
            send_sem=sib_send.at[route, i], recv_sem=sib_recv.at[route, i],
            device_id={"seq": sibling}, device_id_type=pl.DeviceIdType.MESH,
        )

    steps = range(CHUNKS)
    to_ahead = [w_copy(w_own(i), x, i, 0, ahead) for i in steps]
    to_back = [w_copy(w_own(i), x, i, 1, back) for i in steps]
    onward = [w_copy(w_piece(back, core, i), back, i, 2, ahead) for i in steps]
    passes = [[w_pass(shard, i, r) for i in steps] for r, shard in enumerate((back, ahead, across))]

    infos = exchange(lambda p: info.at[b], lambda me: info.at[me], "seq", n_seq, b, seq_send.at[0], seq_recv.at[0])
    states = exchange(lambda p: s1src.at[p], lambda me: s1.at[me], "seq", n_seq, b, seq_send.at[1], seq_recv.at[1])
    start(infos)
    start(states)
    for i in steps:
        to_ahead[i].start()
        to_back[i].start()
    s1[b] = s1src[b]

    local[4].wait()
    gap = (row_i - col_i).astype(F32)
    seg_row = mm(flags, upper)
    allowed = jnp.logical_and(col_i <= row_i, seg_col == seg_row)
    mask_col[...] = mm((col_i == row_i).astype(F32).astype(BF16), masks, NT)
    for h in range(heads_dev):
        within[h] = jnp.where(allowed, jnp.exp(gap * ells[h]), 0.0)
        opening[h] = jnp.where(seg_col[:, :hd] == 0.0, jnp.exp((place + 1.0) * ells[h][:, :hd]), 0.0)
        scores = mm(head(qb, h), head(kb, h), NT)
        pbuf[h] = (within[h] * scores).astype(BF16)
        inner[h] = mm(pbuf[h], head(vb, h))

    def w_step(i):
        to_ahead[i].wait_recv()
        onward[i].start()
        passes[0][i].start()
        to_back[i].wait_recv()
        passes[1][i].start()

    def gate_part(shard, first=False):
        columns = pl.ds(pl.multiple_of(shard * depth, depth), depth)
        part = mm(hid[:, columns], wbuf[shard])
        gate_acc[...] = part if first else gate_acc[...] + part

    local[5].wait()
    local[6].wait()
    gate_part(x, first=True)
    w_step(0)
    pl.semaphore_wait(ready.at[0], 2)
    wave_signal(2, 1)
    arrived(infos)
    keep = [info[j, 0:1] for j in range(n_seq)]
    cnt[x] = functools.reduce(jnp.add, [info[j, 4:8] for j in range(n_seq)])
    counts = exchange(lambda p: cnt.at[x], lambda me: cnt.at[me], "dp", n_dp, x, dp_send.at[0], dp_recv.at[0])
    start(counts)

    carry = jnp.concatenate(carries, axis=0)

    def scan(source, result, order):
        state = jnp.zeros((heads_dev * rows, hd), F32)
        for j in order:
            result[j] = state.astype(result.dtype)
            state = carry * keep[j] * state + source[j].astype(F32)

    arrived(states)
    scan(s1, s2src, range(n_seq))
    states_in = exchange(lambda p: s2src.at[p], lambda me: s2.at[me], "seq", n_seq, b, seq_send.at[2], seq_recv.at[2])
    start(states_in)
    s2[b] = s2src[b]
    for i in steps[1:]:
        w_step(i)
    local[7].wait()
    pl.semaphore_wait(ready.at[1], 2)
    wave_signal(4, 2)
    arrived(states_in)
    state_in = [unpack(s2, h) for h in range(heads_dev)]
    for h in range(heads_dev):
        inner[h] = inner[h] + opening[h] * times(head(qb, h), state_in[h])
    arrived(passes[1])
    gate_part(back)
    arrived(passes[0])
    gate_part(ahead)
    for i in steps:
        onward[i].wait_recv()
        passes[2][i].start()
    arrived(passes[2])
    gate_part(across)
    arrived(counts)
    count = functools.reduce(jnp.add, [cnt[j] for j in range(n_dp)])[0:1]
    scale = n_dp * n_seq * T / count

    square = jnp.zeros((8, hd), F32)
    for h in range(heads_dev):
        attended = inner[h]
        inv = lax.rsqrt(jnp.mean(attended * attended, axis=-1, keepdims=True) + NORM_EPS)
        normed = attended * inv
        gate = jax.nn.sigmoid(gate_acc[:, h * hd:(h + 1) * hd])
        gated = normed * gate
        errors = gated - head(tb, h).astype(F32)
        masked = mask_col[...] * errors
        square = square + jnp.sum((masked * errors).reshape(T // 8, 8, hd), axis=0)
        grad_gated = scale * masked
        dn = grad_gated * gate
        gated_ref[0, :, h * hd:(h + 1) * hd] = gated.astype(BF16)
        ggate_ref[0, :, h * hd:(h + 1) * hd] = (dn * normed * (1.0 - gate)).astype(BF16)
        product = jnp.mean(dn * normed, axis=-1, keepdims=True)
        gout[h] = (inv * (dn - normed * product)).astype(BF16)
    l1[b] = square
    losses = exchange(lambda p: l1.at[b], lambda me: l1.at[me], "seq", n_seq, b, seq_send.at[3], seq_recv.at[3])
    start(losses)
    pack(g1src, [
        functools.reduce(jnp.add, [mm(part, gout[h], TN) for part in split(head(qb, h).astype(F32) * opening[h])])
        for h in range(heads_dev)
    ])
    grads = exchange(lambda p: g1src.at[p], lambda me: g1.at[me], "seq", n_seq, b, seq_send.at[4], seq_recv.at[4])
    start(grads)
    g1[b] = g1src[b]
    for h in range(heads_dev):
        grad = gout[h]
        mixing = (within[h] * mm(grad, head(vb, h), NT)).astype(BF16)
        carried = times(grad, state_in[h], NT)
        gq_ref[0, :, h * hd:(h + 1) * hd] = (mm(mixing, head(kb, h)) + opening[h] * carried).astype(BF16)
        gkp[h] = mm(mixing, head(qb, h), TN)
        gvp[h] = mm(pbuf[h], grad, TN)
    arrived(losses)
    l2[x] = functools.reduce(jnp.add, [l1[j] for j in range(n_seq)])
    losses_dp = exchange(lambda p: l2.at[x], lambda me: l2.at[me], "dp", n_dp, x, dp_send.at[1], dp_recv.at[1])
    start(losses_dp)
    arrived(grads)
    scan(g1, g2src, range(n_seq - 1, -1, -1))
    states_after = exchange(lambda p: g2src.at[p], lambda me: g2.at[me], "seq", n_seq, b, seq_send.at[5], seq_recv.at[5])
    start(states_after)
    g2[b] = g2src[b]
    arrived(losses_dp)
    l3[z] = functools.reduce(jnp.add, [l2[j] for j in range(n_dp)])
    pl.semaphore_wait(ready.at[2], 2)
    losses_z = exchange(lambda p: l3.at[z], lambda me: l3.at[me], "heads", n_heads, z, z_send, z_recv)
    start(losses_z)
    arrived(states_after)
    for h in range(heads_dev):
        after = unpack(g2, h)
        gk_ref[0, :, h * hd:(h + 1) * hd] = (gkp[h] + closing[h] * times(head(vb, h), after, NT)).astype(BF16)
        gv_ref[0, :, h * hd:(h + 1) * hd] = (gvp[h] + closing[h] * times(head(kb, h), after)).astype(BF16)
    arrived(losses_z)
    total = functools.reduce(jnp.add, [l3[j] for j in range(n_heads)])
    loss_ref[0, 0] = jnp.sum(total / (2.0 * count * (heads_dev * n_heads * hd)))

    for copies in (to_ahead, to_back, onward, *passes, infos, states, counts, states_in, losses, grads, losses_dp, states_after, losses_z):
        sent(copies)


def deliver(*refs):
    *arrays, sems = refs
    copies = [pltpu.make_async_copy(arrays[i], arrays[i + 5], sems.at[i]) for i in range(5)]
    start(copies)
    for copy in copies:
        copy.wait()


def local_step(sizes, hidden, w_gate, query_rows, key_rows, value_rows, target, decay_index, loss_mask, doc_reset):
    n_dp, n_seq, n_heads = sizes
    T, D = hidden.shape[1:]
    depth, width = w_gate.shape
    heads_dev = decay_index.shape[0]
    hd = width // heads_dev
    rows = hd // n_seq
    any_spec = pl.BlockSpec(memory_space=pl.ANY)
    out = jax.ShapeDtypeStruct((1, T, width), BF16)
    held = pltpu.VMEM((1, T, width), BF16)
    state = pltpu.VMEM((n_seq, heads_dev * rows, hd), STATE)
    scratch = [
        pltpu.VMEM((T, D), BF16), pltpu.VMEM((n_dp, depth, width), BF16),
        *[pltpu.VMEM((T, width), BF16)] * 4,
        pltpu.VMEM((1, T), jnp.int32), pltpu.VMEM((1, T), jnp.int32), pltpu.VMEM((T, width), F32), pltpu.VMEM((T, hd), F32),
        pltpu.VMEM((heads_dev, T, T), F32), pltpu.VMEM((heads_dev, T, T), BF16),
        pltpu.VMEM((heads_dev, T, hd), F32), pltpu.VMEM((heads_dev, T, hd), F32), pltpu.VMEM((heads_dev, T, hd), F32),
        pltpu.VMEM((heads_dev, T, hd), BF16), pltpu.VMEM((heads_dev, T, hd), F32), pltpu.VMEM((heads_dev, T, hd), F32),
        pltpu.VMEM((n_seq, 8, hd), F32), pltpu.VMEM((n_dp, 4, hd), F32),
        pltpu.VMEM((n_seq, 8, hd), F32), pltpu.VMEM((n_dp, 8, hd), F32), pltpu.VMEM((n_heads, 8, hd), F32),
        *[state] * 8,
        pltpu.SemaphoreType.DMA((8,)),
        pltpu.SemaphoreType.DMA((3, CHUNKS)), pltpu.SemaphoreType.DMA((3, CHUNKS)),
        pltpu.SemaphoreType.DMA((3, CHUNKS)), pltpu.SemaphoreType.DMA((3, CHUNKS)),
        pltpu.SemaphoreType.DMA((6, n_seq)), pltpu.SemaphoreType.DMA((6, n_seq)),
        pltpu.SemaphoreType.DMA((2, n_dp)), pltpu.SemaphoreType.DMA((2, n_dp)),
        pltpu.SemaphoreType.DMA((n_heads,)), pltpu.SemaphoreType.DMA((n_heads,)), pltpu.SemaphoreType.REGULAR((3,)),
    ]
    vmem, smem = pl.BlockSpec(memory_space=pltpu.VMEM), pl.BlockSpec(memory_space=pltpu.SMEM)
    *results, loss = pl.pallas_call(
        functools.partial(kernel, n_dp, n_seq, n_heads),
        out_shape=[held] * 5 + [jax.ShapeDtypeStruct((1, 1), F32)],
        in_specs=[smem] + [any_spec] * 8,
        out_specs=[vmem] * 5 + [smem],
        scratch_shapes=scratch,
        compiler_params=pltpu.CompilerParams(collective_id=0, has_side_effects=True),
        name="layer",
    )(decay_index, loss_mask, doc_reset, hidden, w_gate, query_rows, key_rows, value_rows, target)
    results = pl.pallas_call(
        deliver,
        out_shape=[out] * 5,
        in_specs=[vmem] * 5,
        out_specs=[any_spec] * 5,
        scratch_shapes=[pltpu.SemaphoreType.DMA((5,))],
        name="deliver",
    )(*[pltpu.with_memory_space_constraint(r, pltpu.VMEM) for r in results])
    return (*results, loss.reshape(()))


def solution(mesh):
    sizes = tuple(mesh.shape[a] for a in ("dp", "seq", "heads"))
    rows = P("dp", "seq", "heads")
    return jax.shard_map(
        functools.partial(local_step, sizes),
        mesh=mesh,
        in_specs=(P("dp", "seq", None), P("dp", "heads"), rows, rows, rows, rows, P("heads"), P("dp", "seq"), P("dp", "seq")),
        out_specs=(rows, rows, rows, rows, rows, P()),
        check_vma=False,
    )
```

```python
import functools

import jax
import jax.numpy as jnp
import numpy as np
from jax import lax
from jax.experimental import pallas as pl
from jax.experimental.pallas import tpu as pltpu
from jax.sharding import PartitionSpec as P

TABLE = 16
NORM_EPS = 1e-06
CHUNKS = 3
STATE = jnp.bfloat16
F32, BF16 = jnp.float32, jnp.bfloat16
NN, NT, TN = ((1,), (0,)), ((1,), (1,)), ((0,), (0,))


def mm(a, b, dims=NN):
    return lax.dot_general(a, b, (dims, ((), ())), preferred_element_type=F32)


def split(x):
    hi = x.astype(BF16)
    return hi, (x - hi.astype(F32)).astype(BF16)


def farthest_first(n):
    return sorted(range(1, n), key=lambda d: -min(d, n - d))


def exchange(src, dst, axis, n, me, send, recv):
    copies = []
    for d in farthest_first(n):
        peer = lax.rem(me + d, n)
        copies.append(
            pltpu.make_async_remote_copy(
                src_ref=src(peer),
                dst_ref=dst(me),
                send_sem=send.at[d],
                recv_sem=recv.at[d],
                device_id={axis: peer},
                device_id_type=pl.DeviceIdType.MESH,
            )
        )
    return copies


def signal(sem, axis, peer):
    pl.semaphore_signal(sem, inc=1, device_id={axis: peer}, device_id_type=pl.DeviceIdType.MESH)


def start(copies):
    for copy in copies:
        copy.start()


def arrived(copies):
    for copy in copies:
        copy.wait_recv()


def sent(copies):
    for copy in copies:
        copy.wait_send()


def kernel(
    n_dp, n_seq, n_heads,
    idx_hbm, mask_hbm, reset_hbm, hid_hbm, w_hbm, q_hbm, k_hbm, v_hbm, t_hbm,
    gated_ref, ggate_ref, gq_ref, gk_ref, gv_ref, loss_ref,
    idx, hid, wbuf, qb, kb, vb, tb, mk, rs, gate_acc, mask_col,
    within, pbuf, opening, closing, inner, gout, gkp, gvp,
    info, cnt, l1, l2, l3, s1src, s1, s2src, s2, g1src, g1, g2src, g2,
    loc, w_send, w_recv, seq_send, seq_recv, dp_send, dp_recv, z_send, z_recv, ready,
):
    x, b, z = lax.axis_index("dp"), lax.axis_index("seq"), lax.axis_index("heads")
    T = qb.shape[0]
    hd = gout.shape[2]
    heads_dev = gout.shape[0]
    depth = w_hbm.shape[0]
    piece = depth // 4 // CHUNKS
    rows = hd // n_seq
    core = lax.rem(b, 2)
    sibling = b + 1 - 2 * core
    ahead = lax.rem(x + 1 + 2 * core, n_dp)
    back = lax.rem(x + 3 - 2 * core, n_dp)
    across = lax.rem(x + 2, n_dp)
    row = b // 2
    beside = 2 * lax.rem(row + n_seq // 2 - 1 + 2 * core, n_seq // 2) + core
    quarter = 2 * lax.rem(row, 2) + core
    other = 2 * (1 - lax.rem(row, 2)) + core

    local = [
        pltpu.make_async_copy(s, d, loc.at[i])
        for i, (s, d) in enumerate((
            (reset_hbm, rs), (idx_hbm, idx), (k_hbm.at[0], kb), (v_hbm.at[0], vb), (mask_hbm, mk), (q_hbm.at[0], qb),
            (w_hbm, wbuf.at[x]), (hid_hbm.at[0], hid), (t_hbm.at[0], tb),
        ))
    ]
    start(local[:5])
    barrier = pltpu.get_barrier_semaphore()
    for axis, n, me, reach in (("seq", n_seq, b, n_seq), ("dp", n_dp, x, n_dp), ("heads", n_heads, z, 1)):
        for d in farthest_first(n):
            if min(d, n - d) <= reach:
                signal(barrier, axis, lax.rem(me + d, n))
    start(local[5:])

    local[0].wait()
    local[1].wait()
    local[4].wait()
    row_i = lax.broadcasted_iota(jnp.int32, (T, T), 0)
    col_i = lax.broadcasted_iota(jnp.int32, (T, T), 1)
    lower = (col_i <= row_i).astype(F32).astype(BF16)
    upper = (row_i <= col_i).astype(F32).astype(BF16)
    flags = jnp.broadcast_to(rs[...].astype(F32), (T, T)).astype(BF16)
    seg_col = mm(lower, flags, NT)
    last = seg_col[T - 1:T, :hd]
    masks = jnp.broadcast_to(mk[...].astype(F32), (hd, T)).astype(BF16)
    count_dev = mm(masks[:8], jnp.ones((T, hd), BF16))
    place = row_i[:, :hd].astype(F32)
    fast = float(np.log(np.float32(1.0 / 32.0)))
    slow = float(np.log(np.float32(1.0 / (64.0 * T * n_seq))))
    ells, carries = [], []
    for h in range(heads_dev):
        entry = jnp.full((1, T), idx[h].astype(F32), F32)
        ell = -jnp.exp(fast + entry / (TABLE - 1) * (slow - fast))
        ells.append(ell)
        ell = ell[:, :hd]
        closing[h] = jnp.where(seg_col[:, :hd] == last, jnp.exp((T - 1.0 - place) * ell), 0.0)
        carries.append(jnp.broadcast_to(jnp.exp(T * ell), (rows, hd)))
    info[b, 0:1] = (last == 0.0).astype(F32)
    info[b, 1:2] = count_dev[0:1]

    def head(ref, h):
        return ref[:, h * hd:(h + 1) * hd]

    local[2].wait()
    local[3].wait()
    def pack(ref, parts):
        ref[...] = jnp.concatenate([p.reshape(n_seq, rows, hd) for p in parts], axis=1).astype(ref.dtype)

    def unpack(ref, h):
        state = ref[...].astype(F32)[:, h * rows:(h + 1) * rows].reshape(hd, hd)
        return (state.astype(BF16),) if ref.dtype == BF16 else split(state)

    def times(a, parts, dims=NN):
        return functools.reduce(jnp.add, [mm(a, p, dims) for p in parts])

    pack(s1src, [
        functools.reduce(jnp.add, [mm(part, head(vb, h), TN) for part in split(head(kb, h).astype(F32) * closing[h])])
        for h in range(heads_dev)
    ])

    pl.semaphore_wait(barrier, n_seq + n_dp)

    def wave_signal(d, i):
        for peer in (z + d, z + n_heads - d):
            signal(ready.at[i], "heads", lax.rem(peer, n_heads))

    wave_signal(1, 0)

    def w_piece(shard, part, i):
        return wbuf.at[shard, pl.ds(pl.multiple_of(part * (depth // 4) + i * piece, piece), piece), :]

    def w_copy(kind, route, shard, part, i, target, src=None):
        return pltpu.make_async_remote_copy(
            src_ref=w_piece(shard, part, i) if src is None else src, dst_ref=w_piece(shard, part, i),
            send_sem=w_send.at[kind, route, i], recv_sem=w_recv.at[kind, route, i],
            device_id=target, device_id_type=pl.DeviceIdType.MESH,
        )

    steps = range(CHUNKS)
    own = [w_hbm.at[pl.ds(pl.multiple_of(quarter * (depth // 4) + i * piece, piece), piece), :] for i in steps]
    shards = (back, ahead, across)
    ring = [
        [w_copy(0, 0, x, quarter, i, {"dp": ahead}, own[i]) for i in steps],
        [w_copy(0, 1, x, quarter, i, {"dp": back}, own[i]) for i in steps],
        [w_copy(0, 2, back, quarter, i, {"dp": ahead}) for i in steps],
    ]
    share = [[w_copy(1, r, shards[r], quarter, i, {"seq": sibling}) for i in steps] for r in range(3)]
    step_y = [[w_copy(2, r, shards[r], quarter, i, {"seq": beside}) for i in steps] for r in range(3)]
    relay = [[w_copy(3, r, shards[r], other, i, {"seq": sibling}) for i in steps] for r in range(3)]

    def from_ring(r, i):
        ring[r][i].wait_recv()
        if r == 0:
            ring[2][i].start()
        step_y[r][i].start()
        share[r][i].start()

    def from_side(r, i):
        step_y[r][i].wait_recv()
        relay[r][i].start()

    infos = exchange(lambda p: info.at[b], lambda me: info.at[me], "seq", n_seq, b, seq_send.at[0], seq_recv.at[0])
    states = exchange(lambda p: s1src.at[p], lambda me: s1.at[me], "seq", n_seq, b, seq_send.at[1], seq_recv.at[1])
    start(states)
    for i in steps:
        ring[0][i].start()
        ring[1][i].start()
        if i == 0:
            start(infos)
    s1[b] = s1src[b]

    local[5].wait()
    gap = (row_i - col_i).astype(F32)
    seg_row = mm(flags, upper)
    allowed = jnp.logical_and(col_i <= row_i, seg_col == seg_row)
    mask_col[...] = mm((col_i == row_i).astype(F32).astype(BF16), masks, NT)
    for h in range(heads_dev):
        within[h] = jnp.where(allowed, jnp.exp(gap * ells[h]), 0.0)
        opening[h] = jnp.where(seg_col[:, :hd] == 0.0, jnp.exp((place + 1.0) * ells[h][:, :hd]), 0.0)
        scores = mm(head(qb, h), head(kb, h), NT)
        pbuf[h] = (within[h] * scores).astype(BF16)
        inner[h] = mm(pbuf[h], head(vb, h))

    def gate_part(shard, first=False):
        columns = pl.ds(pl.multiple_of(shard * depth, depth), depth)
        part = mm(hid[:, columns], wbuf[shard])
        gate_acc[...] = part if first else gate_acc[...] + part

    local[6].wait()
    local[7].wait()
    gate_part(x, first=True)
    from_ring(0, 0)
    from_ring(1, 0)
    pl.semaphore_wait(ready.at[0], 2)
    wave_signal(2, 1)
    arrived(infos)
    keep = [info[j, 0:1] for j in range(n_seq)]
    cnt[x] = functools.reduce(jnp.add, [info[j, 1:2] for j in range(n_seq)])
    counts = exchange(lambda p: cnt.at[x], lambda me: cnt.at[me], "dp", n_dp, x, dp_send.at[0], dp_recv.at[0])
    start(counts)

    carry = jnp.concatenate(carries, axis=0)

    def scan(source, result, order):
        state = jnp.zeros((heads_dev * rows, hd), F32)
        for j in order:
            result[j] = state.astype(result.dtype)
            state = carry * keep[j] * state + source[j].astype(F32)

    for i in steps[1:-1]:
        from_ring(0, i)
        from_ring(1, i)
    arrived(states)
    scan(s1, s2src, range(n_seq))
    states_in = exchange(lambda p: s2src.at[p], lambda me: s2.at[me], "seq", n_seq, b, seq_send.at[2], seq_recv.at[2])
    start(states_in)
    s2[b] = s2src[b]
    from_ring(0, CHUNKS - 1)
    from_ring(1, CHUNKS - 1)
    local[8].wait()
    pl.semaphore_wait(ready.at[1], 2)
    wave_signal(4, 2)
    for i in steps:
        from_side(0, i)
        from_side(1, i)
        from_ring(2, i)
    for copies in (*share[:2], *relay[:2]):
        arrived(copies)
    gate_part(back)
    gate_part(ahead)
    for i in steps:
        from_side(2, i)
    arrived(states_in)
    state_in = [unpack(s2, h) for h in range(heads_dev)]
    for h in range(heads_dev):
        inner[h] = inner[h] + opening[h] * times(head(qb, h), state_in[h])
    arrived(share[2])
    arrived(relay[2])
    gate_part(across)
    arrived(counts)
    count = functools.reduce(jnp.add, [cnt[j] for j in range(n_dp)])
    scale = n_dp * n_seq * T / count

    square = jnp.zeros((1, hd), F32)
    invs = []
    for h in range(heads_dev):
        attended = inner[h]
        inv = lax.rsqrt(jnp.mean(attended * attended, axis=-1, keepdims=True) + NORM_EPS)
        normed = attended * inv
        gate = jax.nn.sigmoid(gate_acc[:, h * hd:(h + 1) * hd])
        gated = normed * gate
        errors = gated - head(tb, h).astype(F32)
        square = square + jnp.sum(mask_col[...] * errors * errors, axis=0, keepdims=True)
        gated_ref[0, :, h * hd:(h + 1) * hd] = gated.astype(BF16)
        inner[h] = normed
        gate_acc[:, h * hd:(h + 1) * hd] = gate
        invs.append(inv)
    l1[b] = square
    losses = exchange(lambda p: l1.at[b], lambda me: l1.at[me], "seq", n_seq, b, seq_send.at[3], seq_recv.at[3])
    start(losses)
    for h in range(heads_dev):
        normed, gate = inner[h], gate_acc[:, h * hd:(h + 1) * hd]
        grad_gated = scale * (mask_col[...] * (normed * gate - head(tb, h).astype(F32)))
        dn = grad_gated * gate
        product = jnp.mean(dn * normed, axis=-1, keepdims=True)
        gout[h] = (invs[h] * (dn - normed * product)).astype(BF16)
        ggate_ref[0, :, h * hd:(h + 1) * hd] = (dn * normed * (1.0 - gate)).astype(BF16)
    pack(g1src, [
        functools.reduce(jnp.add, [mm(part, gout[h], TN) for part in split(head(qb, h).astype(F32) * opening[h])])
        for h in range(heads_dev)
    ])
    grads = exchange(lambda p: g1src.at[p], lambda me: g1.at[me], "seq", n_seq, b, seq_send.at[4], seq_recv.at[4])
    start(grads)
    g1[b] = g1src[b]
    for h in range(heads_dev):
        grad = gout[h]
        mixing = (within[h] * mm(grad, head(vb, h), NT)).astype(BF16)
        carried = times(grad, state_in[h], NT)
        gq_ref[0, :, h * hd:(h + 1) * hd] = (mm(mixing, head(kb, h)) + opening[h] * carried).astype(BF16)
        gkp[h] = mm(mixing, head(qb, h), TN)
        gvp[h] = mm(pbuf[h], grad, TN)
    arrived(losses)
    l2[x] = functools.reduce(jnp.add, [l1[j] for j in range(n_seq)])
    for copies in (*ring, *share, *step_y, *relay, infos, states, counts, states_in):
        sent(copies)
    losses_dp = exchange(lambda p: l2.at[x], lambda me: l2.at[me], "dp", n_dp, x, dp_send.at[1], dp_recv.at[1])
    start(losses_dp)
    arrived(grads)
    scan(g1, g2src, range(n_seq - 1, -1, -1))
    states_after = exchange(lambda p: g2src.at[p], lambda me: g2.at[me], "seq", n_seq, b, seq_send.at[5], seq_recv.at[5])
    start(states_after)
    g2[b] = g2src[b]
    arrived(losses_dp)
    l3[z] = functools.reduce(jnp.add, [l2[j] for j in range(n_dp)])
    pl.semaphore_wait(ready.at[2], 2)
    losses_z = exchange(lambda p: l3.at[z], lambda me: l3.at[me], "heads", n_heads, z, z_send, z_recv)
    start(losses_z)
    sent(grads)
    arrived(states_after)
    for h in range(heads_dev):
        after = unpack(g2, h)
        gk_ref[0, :, h * hd:(h + 1) * hd] = (gkp[h] + closing[h] * times(head(vb, h), after, NT)).astype(BF16)
        gv_ref[0, :, h * hd:(h + 1) * hd] = (gvp[h] + closing[h] * times(head(kb, h), after)).astype(BF16)
    arrived(losses_z)
    total = functools.reduce(jnp.add, [l3[j] for j in range(n_heads)])
    loss_ref[...] = total / (2.0 * count * (heads_dev * n_heads * hd))
    for copies in (losses, losses_dp, states_after, losses_z):
        sent(copies)


def deliver(*refs):
    *arrays, loss, sems = refs
    loss[0, 0] = jnp.sum(arrays[5][...])
    arrays[5] = loss
    copies = [pltpu.make_async_copy(arrays[i], arrays[i + 6], sems.at[i]) for i in range(6)]
    start(copies)
    for copy in copies:
        copy.wait()


def local_step(sizes, hidden, w_gate, query_rows, key_rows, value_rows, target, decay_index, loss_mask, doc_reset):
    n_dp, n_seq, n_heads = sizes
    T, D = hidden.shape[1:]
    depth, width = w_gate.shape
    heads_dev = decay_index.shape[0]
    hd = width // heads_dev
    rows = hd // n_seq
    any_spec = pl.BlockSpec(memory_space=pl.ANY)
    out = jax.ShapeDtypeStruct((1, T, width), BF16)
    held = pltpu.VMEM((1, T, width), BF16)
    state = pltpu.VMEM((n_seq, heads_dev * rows, hd), STATE)
    scratch = [
        pltpu.SMEM((heads_dev,), jnp.int32),
        pltpu.VMEM((T, D), BF16), pltpu.VMEM((n_dp, depth, width), BF16),
        *[pltpu.VMEM((T, width), BF16)] * 4,
        pltpu.VMEM((1, T), jnp.int32), pltpu.VMEM((1, T), jnp.int32), pltpu.VMEM((T, width), F32), pltpu.VMEM((T, hd), F32),
        pltpu.VMEM((heads_dev, T, T), F32), pltpu.VMEM((heads_dev, T, T), BF16),
        pltpu.VMEM((heads_dev, T, hd), F32), pltpu.VMEM((heads_dev, T, hd), F32), pltpu.VMEM((heads_dev, T, hd), F32),
        pltpu.VMEM((heads_dev, T, hd), BF16), pltpu.VMEM((heads_dev, T, hd), F32), pltpu.VMEM((heads_dev, T, hd), F32),
        pltpu.VMEM((n_seq, 2, hd), F32), pltpu.VMEM((n_dp, 1, hd), F32),
        pltpu.VMEM((n_seq, 1, hd), F32), pltpu.VMEM((n_dp, 1, hd), F32), pltpu.VMEM((n_heads, 1, hd), F32),
        *[state] * 8,
        pltpu.SemaphoreType.DMA((9,)),
        pltpu.SemaphoreType.DMA((4, 3, CHUNKS)), pltpu.SemaphoreType.DMA((4, 3, CHUNKS)),
        pltpu.SemaphoreType.DMA((6, n_seq)), pltpu.SemaphoreType.DMA((6, n_seq)),
        pltpu.SemaphoreType.DMA((2, n_dp)), pltpu.SemaphoreType.DMA((2, n_dp)),
        pltpu.SemaphoreType.DMA((n_heads,)), pltpu.SemaphoreType.DMA((n_heads,)), pltpu.SemaphoreType.REGULAR((3,)),
    ]
    vmem = pl.BlockSpec(memory_space=pltpu.VMEM)
    results = pl.pallas_call(
        functools.partial(kernel, n_dp, n_seq, n_heads),
        out_shape=[held] * 5 + [pltpu.VMEM((1, hd), F32)],
        in_specs=[any_spec] * 9,
        out_specs=[vmem] * 6,
        scratch_shapes=scratch,
        compiler_params=pltpu.CompilerParams(collective_id=0, has_side_effects=True),
        name="layer",
    )(decay_index, loss_mask, doc_reset, hidden, w_gate, query_rows, key_rows, value_rows, target)
    *results, loss = pl.pallas_call(
        deliver,
        out_shape=[out] * 5 + [jax.ShapeDtypeStruct((1, 1), F32)],
        in_specs=[vmem] * 6,
        out_specs=[any_spec] * 6,
        scratch_shapes=[pltpu.SMEM((1, 1), F32), pltpu.SemaphoreType.DMA((6,))],
        name="deliver",
    )(*[pltpu.with_memory_space_constraint(r, pltpu.VMEM) for r in results])
    return (*results, loss.reshape(()))


def solution(mesh):
    sizes = tuple(mesh.shape[a] for a in ("dp", "seq", "heads"))
    rows = P("dp", "seq", "heads")
    return jax.shard_map(
        functools.partial(local_step, sizes),
        mesh=mesh,
        in_specs=(P("dp", "seq", None), P("dp", "heads"), rows, rows, rows, rows, P("heads"), P("dp", "seq"), P("dp", "seq")),
        out_specs=(rows, rows, rows, rows, rows, P()),
        check_vma=False,
    )
```

```python
import functools

import jax
import jax.numpy as jnp
import numpy as np
from jax import lax
from jax.experimental import pallas as pl
from jax.experimental.pallas import tpu as pltpu
from jax.sharding import PartitionSpec as P

TABLE = 16
NORM_EPS = 1e-06
SHARED, ALONE = 1, 2
STATE = jnp.bfloat16
F32, BF16 = jnp.float32, jnp.bfloat16
NN, NT, TN = ((1,), (0,)), ((1,), (1,)), ((0,), (0,))


def mm(a, b, dims=NN):
    return lax.dot_general(a, b, (dims, ((), ())), preferred_element_type=F32)


def split(x):
    hi = x.astype(BF16)
    return hi, (x - hi.astype(F32)).astype(BF16)


def farthest_first(n):
    return sorted(range(1, n), key=lambda d: -min(d, n - d))


def exchange(src, dst, axis, n, me, send, recv):
    copies = []
    for d in farthest_first(n):
        peer = lax.rem(me + d, n)
        copies.append(
            pltpu.make_async_remote_copy(
                src_ref=src(peer),
                dst_ref=dst(me),
                send_sem=send.at[d],
                recv_sem=recv.at[d],
                device_id={axis: peer},
                device_id_type=pl.DeviceIdType.MESH,
            )
        )
    return copies


def signal(sem, axis, peer):
    pl.semaphore_signal(sem, inc=1, device_id={axis: peer}, device_id_type=pl.DeviceIdType.MESH)


def start(copies):
    for copy in copies:
        copy.start()


def arrived(copies):
    for copy in copies:
        copy.wait_recv()


def sent(copies):
    for copy in copies:
        copy.wait_send()


def kernel(
    n_dp, n_seq, n_heads,
    idx_hbm, mask_hbm, reset_hbm, hid_hbm, w_hbm, q_hbm, k_hbm, v_hbm, t_hbm,
    gated_ref, ggate_ref, gq_ref, gk_ref, gv_ref, loss_ref,
    idx, hid, wbuf, qb, kb, vb, tb, mk, rs, gate_acc, mask_col,
    within, pbuf, opening, closing, inner, gout, gkp, gvp,
    info, cnt, l1, l2, l3, s1src, s1, s2src, s2, g1src, g1, g2src, g2,
    loc, w_send, w_recv, seq_send, seq_recv, dp_send, dp_recv, z_send, z_recv, ready,
):
    x, b, z = lax.axis_index("dp"), lax.axis_index("seq"), lax.axis_index("heads")
    T = qb.shape[0]
    hd = gout.shape[2]
    heads_dev = gout.shape[0]
    depth = w_hbm.shape[0]
    piece = depth // (4 * SHARED + 2 * ALONE)
    rows = hd // n_seq
    core = lax.rem(b, 2)
    sibling = b + 1 - 2 * core
    ahead = lax.rem(x + 1 + 2 * core, n_dp)
    back = lax.rem(x + 3 - 2 * core, n_dp)
    across = lax.rem(x + 2, n_dp)
    row = b // 2
    beside = 2 * lax.rem(row + n_seq // 2 - 1 + 2 * core, n_seq // 2) + core
    quarter = 2 * lax.rem(row, 2) + core
    other = 2 * (1 - lax.rem(row, 2)) + core

    local = [
        pltpu.make_async_copy(s, d, loc.at[i])
        for i, (s, d) in enumerate((
            (reset_hbm, rs), (idx_hbm, idx), (k_hbm.at[0], kb), (v_hbm.at[0], vb), (mask_hbm, mk), (q_hbm.at[0], qb),
            (w_hbm, wbuf.at[x]), (hid_hbm.at[0], hid), (t_hbm.at[0], tb),
        ))
    ]
    start(local[:5])
    barrier = pltpu.get_barrier_semaphore()
    for axis, n, me, reach in (("seq", n_seq, b, n_seq), ("dp", n_dp, x, n_dp), ("heads", n_heads, z, 1)):
        for d in farthest_first(n):
            if min(d, n - d) <= reach:
                signal(barrier, axis, lax.rem(me + d, n))
    start(local[5:])

    local[0].wait()
    local[1].wait()
    local[4].wait()
    row_i = lax.broadcasted_iota(jnp.int32, (T, T), 0)
    col_i = lax.broadcasted_iota(jnp.int32, (T, T), 1)
    lower = (col_i <= row_i).astype(F32).astype(BF16)
    upper = (row_i <= col_i).astype(F32).astype(BF16)
    flags = jnp.broadcast_to(rs[...].astype(F32), (T, T)).astype(BF16)
    seg_col = mm(lower, flags, NT)
    last = seg_col[T - 1:T, :hd]
    masks = jnp.broadcast_to(mk[...].astype(F32), (hd, T)).astype(BF16)
    count_dev = mm(masks[:8], jnp.ones((T, hd), BF16))
    place = row_i[:, :hd].astype(F32)
    fast = float(np.log(np.float32(1.0 / 32.0)))
    slow = float(np.log(np.float32(1.0 / (64.0 * T * n_seq))))
    ells, carries = [], []
    for h in range(heads_dev):
        entry = jnp.full((1, T), idx[h].astype(F32), F32)
        ell = -jnp.exp(fast + entry / (TABLE - 1) * (slow - fast))
        ells.append(ell)
        ell = ell[:, :hd]
        closing[h] = jnp.where(seg_col[:, :hd] == last, jnp.exp((T - 1.0 - place) * ell), 0.0)
        carries.append(jnp.broadcast_to(jnp.exp(T * ell), (rows, hd)))
    info[b, 0:1] = (last == 0.0).astype(F32)
    info[b, 1:2] = count_dev[0:1]

    def head(ref, h):
        return ref[:, h * hd:(h + 1) * hd]

    local[2].wait()
    local[3].wait()
    def pack(ref, parts):
        ref[...] = jnp.concatenate([p.reshape(n_seq, rows, hd) for p in parts], axis=1).astype(ref.dtype)

    def unpack(ref, h):
        state = ref[...].astype(F32)[:, h * rows:(h + 1) * rows].reshape(hd, hd)
        return (state.astype(BF16),) if ref.dtype == BF16 else split(state)

    def times(a, parts, dims=NN):
        return functools.reduce(jnp.add, [mm(a, p, dims) for p in parts])

    pack(s1src, [
        functools.reduce(jnp.add, [mm(part, head(vb, h), TN) for part in split(head(kb, h).astype(F32) * closing[h])])
        for h in range(heads_dev)
    ])

    pl.semaphore_wait(barrier, n_seq + n_dp)

    def wave_signal(d, i):
        for peer in (z + d, z + n_heads - d):
            signal(ready.at[i], "heads", lax.rem(peer, n_heads))

    wave_signal(1, 0)

    def w_rows(part, i):
        first = part * SHARED + i if i < SHARED else 4 * SHARED + core * ALONE + i - SHARED
        return pl.ds(pl.multiple_of(first * piece, piece), piece)

    def w_copy(kind, route, shard, part, i, target, src=None):
        rows_at = wbuf.at[shard, w_rows(part, i), :]
        return pltpu.make_async_remote_copy(
            src_ref=rows_at if src is None else src, dst_ref=rows_at,
            send_sem=w_send.at[kind, route, i], recv_sem=w_recv.at[kind, route, i],
            device_id=target, device_id_type=pl.DeviceIdType.MESH,
        )

    steps, shared = range(SHARED + ALONE), range(SHARED)
    own = [w_hbm.at[w_rows(quarter, i), :] for i in steps]
    shards = (back, ahead, across)
    ring = [
        [w_copy(0, 0, x, quarter, i, {"dp": ahead}, own[i]) for i in steps],
        [w_copy(0, 1, x, quarter, i, {"dp": back}, own[i]) for i in steps],
        [w_copy(0, 2, back, quarter, i, {"dp": ahead}) for i in steps],
    ]
    share = [[w_copy(1, r, shards[r], quarter, i, {"seq": sibling}) for i in steps] for r in range(3)]
    step_y = [[w_copy(2, r, shards[r], quarter, i, {"seq": beside}) for i in shared] for r in range(3)]
    relay = [[w_copy(3, r, shards[r], other, i, {"seq": sibling}) for i in shared] for r in range(3)]

    def from_ring(r, i):
        ring[r][i].wait_recv()
        if r == 0:
            ring[2][i].start()
        if i < SHARED:
            step_y[r][i].start()
        share[r][i].start()

    def from_side(r, i):
        step_y[r][i].wait_recv()
        relay[r][i].start()

    infos = exchange(lambda p: info.at[b], lambda me: info.at[me], "seq", n_seq, b, seq_send.at[0], seq_recv.at[0])
    states = exchange(lambda p: s1src.at[p], lambda me: s1.at[me], "seq", n_seq, b, seq_send.at[1], seq_recv.at[1])
    start(states)
    for i in steps:
        ring[0][i].start()
        ring[1][i].start()
        if i == 0:
            start(infos)
    s1[b] = s1src[b]

    local[5].wait()
    gap = (row_i - col_i).astype(F32)
    seg_row = mm(flags, upper)
    allowed = jnp.logical_and(col_i <= row_i, seg_col == seg_row)
    mask_col[...] = mm((col_i == row_i).astype(F32).astype(BF16), masks, NT)
    for h in range(heads_dev):
        within[h] = jnp.where(allowed, jnp.exp(gap * ells[h]), 0.0)
        opening[h] = jnp.where(seg_col[:, :hd] == 0.0, jnp.exp((place + 1.0) * ells[h][:, :hd]), 0.0)
        scores = mm(head(qb, h), head(kb, h), NT)
        pbuf[h] = (within[h] * scores).astype(BF16)
        inner[h] = mm(pbuf[h], head(vb, h))

    def gate_part(shard, first=False):
        columns = pl.ds(pl.multiple_of(shard * depth, depth), depth)
        part = mm(hid[:, columns], wbuf[shard])
        gate_acc[...] = part if first else gate_acc[...] + part

    local[6].wait()
    local[7].wait()
    gate_part(x, first=True)
    from_ring(0, 0)
    from_ring(1, 0)
    pl.semaphore_wait(ready.at[0], 2)
    wave_signal(2, 1)
    arrived(infos)
    keep = [info[j, 0:1] for j in range(n_seq)]
    cnt[x] = functools.reduce(jnp.add, [info[j, 1:2] for j in range(n_seq)])
    counts = exchange(lambda p: cnt.at[x], lambda me: cnt.at[me], "dp", n_dp, x, dp_send.at[0], dp_recv.at[0])
    start(counts)

    carry = jnp.concatenate(carries, axis=0)

    def scan(source, result, order):
        state = jnp.zeros((heads_dev * rows, hd), F32)
        for j in order:
            result[j] = state.astype(result.dtype)
            state = carry * keep[j] * state + source[j].astype(F32)

    for i in steps[1:SHARED]:
        from_ring(0, i)
        from_ring(1, i)
    arrived(states)
    scan(s1, s2src, range(n_seq))
    states_in = exchange(lambda p: s2src.at[p], lambda me: s2.at[me], "seq", n_seq, b, seq_send.at[2], seq_recv.at[2])
    start(states_in)
    s2[b] = s2src[b]
    from_ring(0, SHARED)
    from_ring(1, SHARED)
    local[8].wait()
    pl.semaphore_wait(ready.at[1], 2)
    wave_signal(4, 2)
    for i in shared:
        from_side(0, i)
        from_side(1, i)
        from_ring(2, i)
    for i in steps[SHARED + 1:]:
        from_ring(0, i)
        from_ring(1, i)
    for i in shared:
        from_side(2, i)
    for i in steps[SHARED:]:
        from_ring(2, i)
    for copies in (*share[:2], *relay[:2]):
        arrived(copies)
    gate_part(back)
    gate_part(ahead)
    arrived(states_in)
    state_in = [unpack(s2, h) for h in range(heads_dev)]
    for h in range(heads_dev):
        inner[h] = inner[h] + opening[h] * times(head(qb, h), state_in[h])
    arrived(share[2])
    arrived(relay[2])
    gate_part(across)
    arrived(counts)
    count = functools.reduce(jnp.add, [cnt[j] for j in range(n_dp)])
    scale = n_dp * n_seq * T / count

    square = jnp.zeros((1, hd), F32)
    invs = []
    for h in range(heads_dev):
        attended = inner[h]
        inv = lax.rsqrt(jnp.mean(attended * attended, axis=-1, keepdims=True) + NORM_EPS)
        normed = attended * inv
        gate = jax.nn.sigmoid(gate_acc[:, h * hd:(h + 1) * hd])
        gated = normed * gate
        errors = gated - head(tb, h).astype(F32)
        square = square + jnp.sum(mask_col[...] * errors * errors, axis=0, keepdims=True)
        gated_ref[0, :, h * hd:(h + 1) * hd] = gated.astype(BF16)
        inner[h] = normed
        gate_acc[:, h * hd:(h + 1) * hd] = gate
        invs.append(inv)
    l1[b] = square
    losses = exchange(lambda p: l1.at[b], lambda me: l1.at[me], "seq", n_seq, b, seq_send.at[3], seq_recv.at[3])
    start(losses)
    for h in range(heads_dev):
        normed, gate = inner[h], gate_acc[:, h * hd:(h + 1) * hd]
        grad_gated = scale * (mask_col[...] * (normed * gate - head(tb, h).astype(F32)))
        dn = grad_gated * gate
        product = jnp.mean(dn * normed, axis=-1, keepdims=True)
        gout[h] = (invs[h] * (dn - normed * product)).astype(BF16)
        ggate_ref[0, :, h * hd:(h + 1) * hd] = (dn * normed * (1.0 - gate)).astype(BF16)
    pack(g1src, [
        functools.reduce(jnp.add, [mm(part, gout[h], TN) for part in split(head(qb, h).astype(F32) * opening[h])])
        for h in range(heads_dev)
    ])
    grads = exchange(lambda p: g1src.at[p], lambda me: g1.at[me], "seq", n_seq, b, seq_send.at[4], seq_recv.at[4])
    start(grads)
    g1[b] = g1src[b]
    for h in range(heads_dev):
        grad = gout[h]
        mixing = (within[h] * mm(grad, head(vb, h), NT)).astype(BF16)
        carried = times(grad, state_in[h], NT)
        gq_ref[0, :, h * hd:(h + 1) * hd] = (mm(mixing, head(kb, h)) + opening[h] * carried).astype(BF16)
        gkp[h] = mm(mixing, head(qb, h), TN)
        gvp[h] = mm(pbuf[h], grad, TN)
    arrived(losses)
    l2[x] = functools.reduce(jnp.add, [l1[j] for j in range(n_seq)])
    losses_dp = exchange(lambda p: l2.at[x], lambda me: l2.at[me], "dp", n_dp, x, dp_send.at[1], dp_recv.at[1])
    start(losses_dp)
    for copies in (*ring, *share, *step_y, *relay, infos, states, counts, states_in):
        sent(copies)
    arrived(grads)
    scan(g1, g2src, range(n_seq - 1, -1, -1))
    states_after = exchange(lambda p: g2src.at[p], lambda me: g2.at[me], "seq", n_seq, b, seq_send.at[5], seq_recv.at[5])
    start(states_after)
    g2[b] = g2src[b]
    arrived(losses_dp)
    l3[z] = functools.reduce(jnp.add, [l2[j] for j in range(n_dp)])
    pl.semaphore_wait(ready.at[2], 2)
    losses_z = exchange(lambda p: l3.at[z], lambda me: l3.at[me], "heads", n_heads, z, z_send, z_recv)
    start(losses_z)
    sent(grads)
    arrived(states_after)
    for h in range(heads_dev):
        after = unpack(g2, h)
        gk_ref[0, :, h * hd:(h + 1) * hd] = (gkp[h] + closing[h] * times(head(vb, h), after, NT)).astype(BF16)
        gv_ref[0, :, h * hd:(h + 1) * hd] = (gvp[h] + closing[h] * times(head(kb, h), after)).astype(BF16)
    arrived(losses_z)
    total = functools.reduce(jnp.add, [l3[j] for j in range(n_heads)])
    loss_ref[...] = total / (2.0 * count * (heads_dev * n_heads * hd))
    for copies in (losses, losses_dp, states_after, losses_z):
        sent(copies)


def deliver(*refs):
    *arrays, loss, sems = refs
    loss[0, 0] = jnp.sum(arrays[5][...])
    arrays[5] = loss
    copies = [pltpu.make_async_copy(arrays[i], arrays[i + 6], sems.at[i]) for i in range(6)]
    start(copies)
    for copy in copies:
        copy.wait()


def local_step(sizes, hidden, w_gate, query_rows, key_rows, value_rows, target, decay_index, loss_mask, doc_reset):
    n_dp, n_seq, n_heads = sizes
    T, D = hidden.shape[1:]
    depth, width = w_gate.shape
    heads_dev = decay_index.shape[0]
    hd = width // heads_dev
    rows = hd // n_seq
    any_spec = pl.BlockSpec(memory_space=pl.ANY)
    out = jax.ShapeDtypeStruct((1, T, width), BF16)
    held = pltpu.VMEM((1, T, width), BF16)
    state = pltpu.VMEM((n_seq, heads_dev * rows, hd), STATE)
    scratch = [
        pltpu.SMEM((heads_dev,), jnp.int32),
        pltpu.VMEM((T, D), BF16), pltpu.VMEM((n_dp, depth, width), BF16),
        *[pltpu.VMEM((T, width), BF16)] * 4,
        pltpu.VMEM((1, T), jnp.int32), pltpu.VMEM((1, T), jnp.int32), pltpu.VMEM((T, width), F32), pltpu.VMEM((T, hd), F32),
        pltpu.VMEM((heads_dev, T, T), F32), pltpu.VMEM((heads_dev, T, T), BF16),
        pltpu.VMEM((heads_dev, T, hd), F32), pltpu.VMEM((heads_dev, T, hd), F32), pltpu.VMEM((heads_dev, T, hd), F32),
        pltpu.VMEM((heads_dev, T, hd), BF16), pltpu.VMEM((heads_dev, T, hd), F32), pltpu.VMEM((heads_dev, T, hd), F32),
        pltpu.VMEM((n_seq, 2, hd), F32), pltpu.VMEM((n_dp, 1, hd), F32),
        pltpu.VMEM((n_seq, 1, hd), F32), pltpu.VMEM((n_dp, 1, hd), F32), pltpu.VMEM((n_heads, 1, hd), F32),
        *[state] * 8,
        pltpu.SemaphoreType.DMA((9,)),
        pltpu.SemaphoreType.DMA((4, 3, SHARED + ALONE)), pltpu.SemaphoreType.DMA((4, 3, SHARED + ALONE)),
        pltpu.SemaphoreType.DMA((6, n_seq)), pltpu.SemaphoreType.DMA((6, n_seq)),
        pltpu.SemaphoreType.DMA((2, n_dp)), pltpu.SemaphoreType.DMA((2, n_dp)),
        pltpu.SemaphoreType.DMA((n_heads,)), pltpu.SemaphoreType.DMA((n_heads,)), pltpu.SemaphoreType.REGULAR((3,)),
    ]
    vmem = pl.BlockSpec(memory_space=pltpu.VMEM)
    results = pl.pallas_call(
        functools.partial(kernel, n_dp, n_seq, n_heads),
        out_shape=[held] * 5 + [pltpu.VMEM((1, hd), F32)],
        in_specs=[any_spec] * 9,
        out_specs=[vmem] * 6,
        scratch_shapes=scratch,
        compiler_params=pltpu.CompilerParams(collective_id=0, has_side_effects=True),
        name="layer",
    )(decay_index, loss_mask, doc_reset, hidden, w_gate, query_rows, key_rows, value_rows, target)
    *results, loss = pl.pallas_call(
        deliver,
        out_shape=[out] * 5 + [jax.ShapeDtypeStruct((1, 1), F32)],
        in_specs=[vmem] * 6,
        out_specs=[any_spec] * 6,
        scratch_shapes=[pltpu.SMEM((1, 1), F32), pltpu.SemaphoreType.DMA((6,))],
        name="deliver",
    )(*[pltpu.with_memory_space_constraint(r, pltpu.VMEM) for r in results])
    return (*results, loss.reshape(()))


def solution(mesh):
    sizes = tuple(mesh.shape[a] for a in ("dp", "seq", "heads"))
    rows = P("dp", "seq", "heads")
    return jax.shard_map(
        functools.partial(local_step, sizes),
        mesh=mesh,
        in_specs=(P("dp", "seq", None), P("dp", "heads"), rows, rows, rows, rows, P("heads"), P("dp", "seq"), P("dp", "seq")),
        out_specs=(rows, rows, rows, rows, rows, P()),
        check_vma=False,
    )
```
